32 devices in a mesh: members: 4 (over y, core), space: 8 (over z, x).
Axes of the slice: x: 2, y: 2, z: 4, core: 2. Of those that a mesh axis runs over, the one named last changes fastest.
Arguments:
- ensemble: float32 [3, 512, 64, 256], P(None, 'members', 'space'), may hold values from -6 to 6
- obs_cells: int32 [8, 4, 128], P('space', 'members'), may hold values from 0 to 1535
- obs_values: float32 [8, 4, 128], P('space', 'members'), may hold values from -6 to 6
- obs_var: float32 [8, 4, 128], P('space', 'members'), may hold values from 0.25 to 4
- obs_noise: float32 [512, 8, 4, 128], P(None, 'space', 'members'), may hold values from -6 to 6
- assign: int32 [512], replicated, may hold values from 0 to 511, each once
Outputs:
- analysis: float32 [3, 512, 64, 256], P(None, 'members', 'space')
The draws below stay inside these ranges and needn't reach their ends.
Inputs may be any that keep to these rules, and one draw needn't show every extreme that they name: assign holds every member once. obs_cells[r, c, k] = field * 8 * 64 + row * 64 + column within tile (r, c); repeats are possible.
All inputs are finite; a program needn't handle non-finite values.
Results may differ from the reference program's by a relative error of at most 0.0003.
Values sent between devices are 32-bit elements; how exact they have to be, the bound alone decides.
A program may use at most 64 MiB of HBM per device.

```python
import math
import jax
import jax.numpy as jnp
from jax import lax

ROWS_DEV = 8
TILE_W = 64
STEPS = 4
OBS_TILE = 128
MEMBERS = 512
TILE_ROWS = 8
TILE_COLS = 4
NX = 256
NY = 64


def touch_ends(entries, own_key, low, top_value):
    extent = entries.shape
    spot = [jax.random.randint(jax.random.fold_in(own_key, axis), (), 0, extent[axis]) for axis in range(len(extent))]
    entries = entries.at[tuple(spot)].set(low)
    longest = extent.index(max(extent))
    spot[longest] = (spot[longest] + 1) % extent[longest]
    return entries.at[tuple(spot)].set(top_value)


def level_of(rng, shape, pieces, smallest, largest):
    gain = 1.0
    for axis_at, parts in pieces:
        heights = jax.random.uniform(jax.random.fold_in(jax.random.fold_in(rng, 6), axis_at), (parts,), jnp.float32, smallest / len(pieces), largest / len(pieces))
        gain = gain * jnp.repeat(jnp.exp(heights), shape[axis_at] // parts).reshape((-1,) + (1,) * (len(shape) - 1 - axis_at))
    return gain


def centred(own_key, shape, width, limit, pieces=(), held_as=jnp.bfloat16):
    factor_of = level_of(own_key, shape, pieces, -0.22, 0.18) if pieces else 1.0
    values = jax.random.normal(own_key, shape, jnp.float32) * width * factor_of
    return jnp.minimum(jnp.maximum(values, -limit), limit).astype(held_as)


def setup_inputs(seed: int = 0) -> dict:
    arg_keys = jax.random.split(jax.random.key(seed), 7)
    return {
        "ensemble": centred(arg_keys[0], (3, MEMBERS, NY, NX), 1.0, 6.0, ((1, 4), (2, 8)), jnp.float32),
        "obs_cells": touch_ends(jax.random.randint(arg_keys[1], (TILE_ROWS, TILE_COLS, OBS_TILE), 0, 3 * ROWS_DEV * TILE_W), jax.random.fold_in(arg_keys[1], 1), 0, (3 * ROWS_DEV * TILE_W) - 1).astype(jnp.int32),
        "obs_values": centred(arg_keys[2], (TILE_ROWS, TILE_COLS, OBS_TILE), 1.0, 6.0, ((0, 8), (1, 4)), jnp.float32),
        "obs_var": jnp.clip(jnp.exp(math.log(4.0) - 2.7725887 * jax.random.uniform(arg_keys[3], (TILE_ROWS, TILE_COLS, OBS_TILE), jnp.float32) ** level_of(arg_keys[3], (TILE_ROWS, TILE_COLS, OBS_TILE), ((0, 8), (1, 4)), -0.2, 0.2)), 0.25, 4.0),
        "obs_noise": centred(arg_keys[4], (MEMBERS, TILE_ROWS, TILE_COLS, OBS_TILE), 1.0, 6.0, ((1, 8), (2, 4)), jnp.float32),
        "assign": jax.random.permutation(arg_keys[5], MEMBERS).astype(jnp.int32),
    }


tstep = 0.1
gravity = 1.0
depth = 1.0
coriolis = 0.25
viscosity = 0.5

def centred_x(field):
    return 0.5 * (jnp.roll(field, -1, axis=2) - jnp.roll(field, 1, axis=2))

def height_update(state):
    eta, east, north = (state[0], state[1], state[2])
    column = depth + eta
    flux_x = centred_x(column * east)[:, 1:-1]
    carried = column * north
    flux_y = 0.5 * (carried[:, 2:] - carried[:, :-2])
    return eta[:, 1:-1] - tstep * (flux_x + flux_y)

def momentum_update(eta, east, north):

    def advance(field, extra):
        inner = field[:, 1:-1]
        grad_x = centred_x(field)[:, 1:-1]
        grad_y = 0.5 * (field[:, 2:] - field[:, :-2])
        spread = jnp.roll(field, -1, axis=2)[:, 1:-1] + jnp.roll(field, 1, axis=2)[:, 1:-1] + field[:, 2:] + field[:, :-2] - 4.0 * inner
        return inner + tstep * (-east[:, 1:-1] * grad_x - north[:, 1:-1] * grad_y + extra + viscosity * spread)
    slope_x = centred_x(eta)[:, 1:-1]
    slope_y = 0.5 * (eta[:, 2:] - eta[:, :-2])
    new_east = advance(east, coriolis * north[:, 1:-1] - gravity * slope_x)
    new_north = advance(north, -coriolis * east[:, 1:-1] - gravity * slope_y)
    return (new_east, new_north)

def pad_rows(state):
    return jnp.concatenate([state[:, :, -1:], state, state[:, :, :1]], axis=2)

def observe(tile, cells, values, variance, noise):
    tile_cells = tile.shape[2]
    field_of = cells // tile_cells
    cell_of = cells % tile_cells
    observed = tile[field_of, :, cell_of].T
    scale = 1.0 / jnp.sqrt(variance)
    mean_obs = lax.optimization_barrier(jnp.mean(observed, axis=0, keepdims=True))
    spread = (observed - mean_obs) * scale
    misfit = (values[None, :] - observed) * scale + noise
    return jnp.stack([spread, misfit])

def analyse_tile(tile, near):
    count = tile.shape[1]
    spread_all = jnp.transpose(near[:, :, 0], (2, 0, 1, 3)).reshape(count, -1)
    misfit_all = jnp.transpose(near[:, :, 1], (2, 0, 1, 3)).reshape(count, -1)
    gram = jnp.dot(spread_all, spread_all.T, precision=lax.Precision.HIGHEST) / (count - 1) + jnp.eye(count, dtype=jnp.float32)
    factor = jnp.linalg.cholesky(gram)
    reduced = jax.scipy.linalg.cho_solve((factor, True), spread_all)
    mixing = jnp.dot(misfit_all, reduced.T, precision=lax.Precision.HIGHEST) / (count - 1)
    anomaly = tile - lax.optimization_barrier(jnp.mean(tile, axis=1, keepdims=True))
    return tile + jnp.einsum('ij,fjc->fic', mixing, anomaly, precision=lax.Precision.HIGHEST)

def reference(ensemble, obs_cells, obs_values, obs_var, obs_noise, assign):
    state = ensemble
    for step in range(STEPS):
        eta_new = height_update(pad_rows(state))
        padded = pad_rows(jnp.stack([eta_new, state[1], state[2]]))
        east, north = momentum_update(padded[0], padded[1], padded[2])
        state = jnp.stack([eta_new, east, north])
    tiles = state.reshape(3, MEMBERS, TILE_ROWS, ROWS_DEV, TILE_COLS, TILE_W)
    tiles = tiles.transpose(2, 4, 0, 1, 3, 5).reshape(TILE_ROWS, TILE_COLS, 3, MEMBERS, ROWS_DEV * TILE_W)
    noise_all = jnp.take(obs_noise, assign, axis=0)
    noise_tiles = jnp.transpose(noise_all, (1, 2, 0, 3))
    packs = jax.vmap(jax.vmap(observe))(tiles, obs_cells, obs_values, obs_var, noise_tiles)

    def one_tile(index):
        row = index // TILE_COLS
        col = index % TILE_COLS
        offsets = jnp.arange(-1, 2, dtype=jnp.int32)
        rows = (row + offsets) % TILE_ROWS
        cols = (col + offsets) % TILE_COLS
        near = jnp.take(jnp.take(packs, rows, axis=0), cols, axis=1)
        return analyse_tile(tiles[row, col], near)
    done = lax.map(one_tile, jnp.arange(TILE_ROWS * TILE_COLS, dtype=jnp.int32))
    done = done.reshape(TILE_ROWS, TILE_COLS, 3, MEMBERS, ROWS_DEV, TILE_W)
    return done.transpose(2, 3, 0, 4, 1, 5).reshape(3, MEMBERS, NY, NX)
```

```python
import functools

import jax
import jax.numpy as jnp
from jax import lax
from jax.experimental import pallas as pl
from jax.experimental.pallas import tpu as pltpu
from jax.sharding import PartitionSpec as P

TILE_W = 64
STEPS = 4
BLOCK = 128

tstep = 0.1
gravity = 1.0
depth = 1.0
coriolis = 0.25
viscosity = 0.5

HIGHEST = lax.Precision.HIGHEST


def forecast_kernel(cols, half, x_ref, y_ref):
    parts, _, _, rows, nx = x_ref.shape
    ny = parts * rows
    member = pl.program_id(0)

    def neighbours(f):
        return (
            pltpu.roll(f, nx - 1, 1),
            pltpu.roll(f, 1, 1),
            pltpu.roll(f, ny - 1, 0),
            pltpu.roll(f, 1, 0),
        )

    eta, east, north = (x_ref[:, f, 0].reshape(ny, nx) for f in range(3))
    for _ in range(STEPS):
        column = depth + eta
        flux = column * east
        carried = column * north
        div = 0.5 * (pltpu.roll(flux, nx - 1, 1) - pltpu.roll(flux, 1, 1)) + 0.5 * (
            pltpu.roll(carried, ny - 1, 0) - pltpu.roll(carried, 1, 0)
        )
        eta = eta - tstep * div
        right, left, below, above = neighbours(eta)
        slope_x = 0.5 * (right - left)
        slope_y = 0.5 * (below - above)

        def advance(field, extra):
            right, left, below, above = neighbours(field)
            grad_x = 0.5 * (right - left)
            grad_y = 0.5 * (below - above)
            lap = right + left + below + above - 4.0 * field
            return field + tstep * (
                -east * grad_x - north * grad_y + extra + viscosity * lap
            )

        new_east = advance(east, coriolis * north - gravity * slope_x)
        new_north = advance(north, -coriolis * east - gravity * slope_y)
        east, north = new_east, new_north

    width = nx // cols
    lane = lax.broadcasted_iota(jnp.int32, (rows, 2 * width), 1)
    low = lane < width
    for f, field in enumerate((eta, east, north)):
        for r in range(parts):
            for p in range(cols // 2):
                v = field[r * rows : (r + 1) * rows, 2 * p * width : 2 * (p + 1) * width]
                turned = pltpu.roll(v, half, 0)
                first = jnp.where(low, v, pltpu.roll(turned, width, 1))
                second = jnp.where(low, pltpu.roll(v, width, 1), turned)
                for q in range(half):
                    y_ref[2 * p, r, f, q, pl.ds(member, 1), :] = first[q : q + 1]
                    y_ref[2 * p + 1, r, f, q, pl.ds(member, 1), :] = second[q : q + 1]


def forecast(x, cols):
    parts, fields, members, rows, nx = x.shape
    half = rows // 2
    return pl.pallas_call(
        functools.partial(forecast_kernel, cols, half),
        grid=(members,),
        in_specs=[pl.BlockSpec((parts, fields, 1, rows, nx), lambda j: (0, 0, j, 0, 0))],
        out_specs=pl.BlockSpec(
            (cols, parts, fields, half, members, 2 * nx // cols), lambda j: (0, 0, 0, 0, 0, 0)
        ),
        out_shape=jax.ShapeDtypeStruct(
            (cols, parts, fields, half, members, 2 * nx // cols), jnp.float32
        ),
        compiler_params=pltpu.CompilerParams(vmem_limit_bytes=48 * 1024 * 1024),
        name="forecast",
    )(x)


def unshuffle_kernel(x_ref, o_ref):
    cols, _, half, slots, lanes = x_ref.shape
    width = lanes // 2
    low = lax.broadcasted_iota(jnp.int32, (slots, lanes), 1) < width
    for q in range(half):
        for p in range(cols // 2):
            first = x_ref[2 * p, 0, q]
            second = x_ref[2 * p + 1, 0, q]
            top = jnp.where(low, first, pltpu.roll(second, width, 1))
            bottom = jnp.where(low, pltpu.roll(first, width, 1), second)
            o_ref[0, :, q, p * lanes : (p + 1) * lanes] = top
            o_ref[0, :, half + q, p * lanes : (p + 1) * lanes] = bottom


def unshuffle(x):
    cols, fields, half, slots, lanes = x.shape
    nx = cols * lanes // 2
    return pl.pallas_call(
        unshuffle_kernel,
        grid=(fields,),
        in_specs=[pl.BlockSpec((cols, 1, half, slots, lanes), lambda f: (0, f, 0, 0, 0))],
        out_specs=pl.BlockSpec((1, slots, 2 * half, nx), lambda f: (f, 0, 0, 0)),
        out_shape=jax.ShapeDtypeStruct((fields, slots, 2 * half, nx), jnp.float32),
        compiler_params=pltpu.CompilerParams(vmem_limit_bytes=32 * 1024 * 1024),
        name="unshuffle",
    )(x)


def dot(a, b):
    return jnp.dot(a, b, precision=HIGHEST, preferred_element_type=jnp.float32)


def inverse_kernel(g_ref, a_ref, d_ref):
    size = g_ref.shape[0]
    a_ref[...] = g_ref[...]
    row_id = lax.broadcasted_iota(jnp.int32, (BLOCK, BLOCK), 0)
    lane_id = lax.broadcasted_iota(jnp.int32, (BLOCK, BLOCK), 1)
    lane_row = lax.broadcasted_iota(jnp.int32, (1, BLOCK), 1)

    def block_step(b, carry):
        at = pl.ds(pl.multiple_of(b * BLOCK, BLOCK), BLOCK)
        d_ref[...] = a_ref[at, at]

        def outer(o, c):
            base = pl.multiple_of(o * 8, 8)
            for i in range(8):
                k = base + i
                a = d_ref[...]
                row = d_ref[pl.ds(k, 1), :]
                col = jnp.sum(jnp.where(lane_id == k, a, 0.0), axis=1, keepdims=True)
                pivot = jnp.sum(jnp.where(lane_row == k, row, 0.0), axis=1, keepdims=True)
                inv = 1.0 / pivot
                scaled = jnp.where(lane_row == k, inv, row * inv)
                kept = jnp.where(lane_id == k, 0.0, a)
                d_ref[...] = jnp.where(row_id == k, scaled, kept - col * scaled)
            return c

        lax.fori_loop(0, BLOCK // 8, outer, 0)
        inv = d_ref[...]
        inv = 0.5 * (inv + inv.T)
        side = a_ref[:, at]
        row = dot(inv, a_ref[at, :])
        back = -dot(side, inv)
        a_ref[...] = a_ref[...] - dot(side, row)
        a_ref[:, at] = back
        a_ref[at, :] = row
        a_ref[at, at] = inv
        return carry

    lax.fori_loop(0, size // BLOCK, block_step, 0)


def inverse(gram):
    size = gram.shape[0]
    return pl.pallas_call(
        inverse_kernel,
        out_shape=jax.ShapeDtypeStruct((size, size), jnp.float32),
        scratch_shapes=[pltpu.VMEM((BLOCK, BLOCK), jnp.float32)],
        cost_estimate=pl.CostEstimate(
            flops=200 * size**3, bytes_accessed=8 * size * size, transcendentals=0
        ),
        compiler_params=pltpu.CompilerParams(vmem_limit_bytes=32 * 1024 * 1024),
        name="inverse",
    )(gram)


def shifted(x, axis):
    count = lax.axis_size(axis)
    up = lax.ppermute(x, axis, [(i, (i + 1) % count) for i in range(count)])
    down = lax.ppermute(x, axis, [((i + 1) % count, i) for i in range(count)])
    return up, down


def nearby(x):
    slots, obs = x.shape
    tall = jnp.concatenate([x, *shifted(x, "space")], axis=1)
    return jnp.concatenate([tall, *shifted(tall, "members")], axis=1)


def local(ensemble, obs_cells, obs_values, obs_var, obs_noise, assign):
    space = lax.axis_size("space")
    cols = lax.axis_size("members")
    fields, here, rows, nx = ensemble.shape
    width = nx // cols
    half = rows // 2
    lanes = 2 * width
    each = here // space

    split = jnp.transpose(ensemble.reshape(fields, space, each, rows, nx), (1, 0, 2, 3, 4))
    whole = lax.all_to_all(split, "space", 0, 0, tiled=True)
    tiles = forecast(whole, cols)
    tiles = tiles.reshape(cols * space, fields * half, each, lanes)
    tiles = lax.all_to_all(tiles, ("members", "space"), 0, 0, tiled=True)
    count = cols * space * each
    tile = jnp.transpose(tiles, (1, 0, 2, 3)).reshape(fields * half, count, lanes)

    cells = obs_cells.reshape(-1)
    field_of = cells // (rows * width)
    row_of = cells // width % rows
    group_of = field_of * half + row_of % half
    lane_of = row_of // half * width + cells % width
    shape = (fields * half, lanes, cells.shape[0])
    pick = (
        (lax.broadcasted_iota(jnp.int32, shape, 0) == group_of[None, None, :])
        & (lax.broadcasted_iota(jnp.int32, shape, 1) == lane_of[None, None, :])
    ).astype(jnp.float32)
    observed = jnp.einsum("gmc,gco->mo", tile, pick, precision=HIGHEST)
    scale = 1.0 / jnp.sqrt(obs_var.reshape(-1))
    mean_obs = jnp.mean(observed, axis=0, keepdims=True)
    spread = (observed - mean_obs) * scale
    noise = jnp.take(obs_noise.reshape(count, -1), assign, axis=0)
    misfit = (obs_values.reshape(-1)[None, :] - observed) * scale + noise

    near = nearby(spread)
    near_misfit = nearby(misfit)
    gram = dot(near, near.T) / (count - 1) + jnp.eye(count, dtype=jnp.float32)
    solved = inverse(gram)
    cross = dot(near_misfit, near.T) / (count - 1)
    mixing = dot(cross, solved)
    anomaly = tile - jnp.mean(tile, axis=1, keepdims=True)
    updated = tile + jnp.einsum("ij,gjc->gic", mixing, anomaly, precision=HIGHEST)

    back = jnp.transpose(updated.reshape(fields * half, cols, here, lanes), (1, 0, 2, 3))
    back = lax.all_to_all(back, "members", 0, 0, tiled=True)
    return unshuffle(back.reshape(cols, fields, half, here, lanes))


def solution(mesh):
    in_specs = (
        P(None, "members", "space", None),
        P("space", "members", None),
        P("space", "members", None),
        P("space", "members", None),
        P(None, "space", "members", None),
        P(),
    )
    out_specs = P(None, "members", "space", None)
    return jax.shard_map(local, mesh=mesh, in_specs=in_specs, out_specs=out_specs, check_vma=False)
```
